256 devices in a mesh: grp: 8 (over z), slab: 32 (over y, x, core).
Axes of the slice: x: 4, y: 4, z: 8, core: 2. Of those that a mesh axis runs over, the one named last changes fastest.
Arguments:
- spectra: bfloat16 [131072, 2048], P(('grp', 'slab')), may hold values from -6 to 6
- ctf_sq: bfloat16 [131072, 1024], P(('grp', 'slab')), may hold values from 0.049804688 to 1
- dest: int32 [131072, 1], P(('grp', 'slab')), may hold values from 0 to 31; in each aligned block of 512 rows (0 to 511, 512 to 1023, ...) at most 32 rows name the same one
- block: int32 [131072], P(('grp', 'slab')), may hold values from 0 to 63
- pattern: int32 [131072], P(('grp', 'slab')), may hold values from 0 to 63
- pattern_table: bfloat16 [64, 8], replicated, may hold values from 0.049804688 to 1
- tau: float32 [1024], replicated, may hold values from 0.5 to 4
Outputs:
- image: float32 [2, 16, 1024, 1024], P(None, 'grp', None, 'slab')
The draws below stay inside these ranges and needn't reach their ends.
Inputs may be any that keep to these rules, and one draw needn't show every extreme that they name: `dest`: among the rows of one device at most 32 name the same slab; in some device's rows one slab is named by exactly 32.
All inputs are finite; a program needn't handle non-finite values.
Results may differ from the reference program's by a relative error of at most 0.0003.
Values may be sent and summed in bfloat16 or wider, within the bound.
A program may use at most 192 MiB of HBM per device.

```python
import math
import jax
import jax.numpy as jnp
import numpy as np
from jax import lax

L = 1024
KZ_DEV = 32
RB = 8
NW = 64
YWIN = 16
ROWS_DEV = 512
CAP = 32
NBLK = 64
NZ = 1024
ROWS = 131072
N_SLAB = 32


def with_ends(entries, rng, smallest, high):
    longest = entries.shape.index(max(entries.shape))
    spots = []
    for shift in (0, 1):
        where = [jax.random.randint(jax.random.fold_in(rng, axis), (), 0, length) for axis, length in enumerate(entries.shape)]
        where[longest] = (where[longest] + shift) % entries.shape[longest]
        spots.append(tuple(where))
    return entries.at[spots[0]].set(smallest).at[spots[1]].set(high)


def level_of(key, dims, cuts, least, top_value):
    def one(position, shards_of):
        steps = jax.random.uniform(jax.random.fold_in(jax.random.fold_in(key, 6), position), (shards_of,), jnp.float32, least / len(cuts), top_value / len(cuts))
        return jnp.repeat(jnp.exp(steps), dims[position] // shards_of).reshape((-1,) + (1,) * (len(dims) - position - 1))

    level = one(*cuts[0])
    for cut in cuts[1:]:
        level = level * one(*cut)
    return level


def deal_out(own_key, own, number, rows, number_of, top, most, lean):
    order = jax.random.permutation(own_key, number_of)
    heavy_load, common = portions_of(number_of, rows * top, most, lean, True), portions_of(number_of, rows * top, most, lean, False)
    places = jnp.arange(number_of)

    def named(lengths, turn):
        used = int((lengths > 0).sum())
        fixed = max(1, used // 4)
        shifted = fixed + (places - fixed + turn * (used - fixed)) % max(1, number_of - fixed)
        return jnp.zeros((number_of,), jnp.int32).at[order[jnp.where(places < fixed, places, shifted)]].set(jnp.asarray(lengths, jnp.int32))

    lengths = jnp.where(number % 4 == 0, named(heavy_load, number // 4), named(common, number - number // 4 - 1))
    mixed = jax.random.permutation(jax.random.fold_in(own, 3), number_of)
    donor, receiver = mixed[0:number_of // 2 * 2:2], mixed[1:number_of // 2 * 2:2]
    slack = jnp.minimum(lengths[donor] - 1, most - lengths[receiver]) // 2
    slack = jnp.where((donor == order[0]) | (receiver == order[0]) | (lengths[receiver] == 0), 0, jnp.maximum(slack, 0))
    shifted = jax.random.randint(jax.random.fold_in(own, 4), (number_of // 2,), 0, 1 << 20) % (slack + 1)
    lengths = lengths.at[donor].add(-shifted).at[receiver].add(shifted)
    labels = jnp.searchsorted(jnp.cumsum(lengths), jnp.arange(rows * top), side="right").astype(jnp.int32)
    listing = labels.reshape(top, rows).T
    listing = listing[jax.random.permutation(jax.random.fold_in(own, 1), rows)]
    turn = jax.random.randint(jax.random.fold_in(own, 2), (rows, 1), 0, top)
    return jnp.take_along_axis(listing, (jnp.arange(top)[None, :] + turn) % top, axis=1)


def portions_of(number_of, total, reach, lean, full):
    loads = [(1 << 20) // math.isqrt(rank ** lean) + 1 for rank in range(1, number_of + 1)]
    largest = reach if full else min(reach, max(-(-total // number_of), total * loads[0] // sum(loads)))
    least = 1 if total - largest >= number_of - 1 else 0
    given, rest = [largest] + [least] * (number_of - 1), total - largest - least * (number_of - 1)
    while rest > 0:
        candidates = [i for i in range(1, number_of) if given[i] < largest] or [i for i in range(1, number_of) if given[i] < reach]
        whole, left = sum([loads[i] for i in candidates]), rest
        for i in candidates:
            addition = min(reach - given[i], max(1, left * loads[i] // whole), rest)
            given[i] = given[i] + addition
            rest = rest - addition
    return np.array(given)


def scatter_about(rng, extent, spread, bound, pieces=(), kind=jnp.bfloat16):
    entries = spread * jax.random.normal(rng, extent, jnp.float32)
    if pieces:
        entries = entries * level_of(rng, extent, pieces, -0.22, 0.18)
    return jnp.clip(entries, -bound, bound).astype(kind)


def setup_inputs(seed: int = 0) -> dict:
    seeds = jax.random.split(jax.random.key(seed), 8)
    spectra = scatter_about(seeds[0], (ROWS, 2 * L), 1.0, 6.0, ((0, 256),))
    ctf_sq = jnp.clip(jnp.exp(math.log(1.0) - 2.9996462 * jax.random.uniform(seeds[1], (ROWS, L), jnp.float32) ** level_of(seeds[1], (ROWS, L), ((0, 256),), -0.2, 0.2)), 0.049804688, 1.0).astype(jnp.bfloat16)
    dest_keys = jax.random.split(jax.random.fold_in(seeds[2], 1), ROWS // ROWS_DEV)
    dest_turns = jax.random.permutation(jax.random.fold_in(seeds[2], 3), ROWS // ROWS_DEV)
    dest = jax.vmap(lambda own, number: deal_out(jax.random.fold_in(seeds[2], 2), own, number, ROWS_DEV, N_SLAB, 1, CAP, 2))(dest_keys, dest_turns).reshape((ROWS, 1))
    block = with_ends(jax.random.randint(seeds[3], (ROWS,), 0, NBLK), jax.random.fold_in(seeds[3], 1), 0, NBLK - 1).astype(jnp.int32)
    pattern = with_ends(jax.random.randint(seeds[4], (ROWS,), 0, NW), jax.random.fold_in(seeds[4], 1), 0, NW - 1).astype(jnp.int32)
    pattern_table = jnp.clip(jax.random.uniform(seeds[5], (NW, RB), jnp.float32, 0.049804688, 1.0), 0.049804688, 1.0).astype(jnp.bfloat16)
    tau = jnp.clip(jnp.exp(jax.random.uniform(seeds[6], (L,), jnp.float32, math.log(0.5), math.log(4.0))), 0.5, 4.0)
    return {"spectra": spectra, "ctf_sq": ctf_sq, "dest": dest, "block": block, "pattern": pattern, "pattern_table": pattern_table, "tau": tau}


def reference(spectra, ctf_sq, dest, block, pattern, pattern_table, tau):
    total_rows = spectra.shape[0]
    step_rows = min(1024, total_rows)
    num_steps = total_rows // step_rows
    table_f = pattern_table.astype(jnp.float32)
    global_block = dest[:, 0] * NBLK + block
    volume_rows = N_SLAB * YWIN * KZ_DEV

    def accumulate(volume, index):
        first_row = (index * step_rows).astype(jnp.int32)
        spec_part = lax.dynamic_slice_in_dim(spectra, first_row, step_rows, 0).astype(jnp.float32)
        ctf_part = lax.dynamic_slice_in_dim(ctf_sq, first_row, step_rows, 0).astype(jnp.float32)
        payload = jnp.concatenate([spec_part, ctf_part], axis=1)
        pattern_part = lax.dynamic_slice_in_dim(pattern, first_row, step_rows, 0)
        block_part = lax.dynamic_slice_in_dim(global_block, first_row, step_rows, 0)
        weights = table_f[pattern_part]
        for inner in range(RB):
            volume = volume.at[block_part * RB + inner].add(weights[:, inner:inner + 1] * payload)
        return volume, None

    start_volume = jnp.zeros((volume_rows, 3 * L), jnp.float32)
    volume, unused = lax.scan(accumulate, start_volume, jnp.arange(num_steps, dtype=jnp.int32))
    volume = volume.reshape(N_SLAB, YWIN, KZ_DEV, 3, L)
    filtered = volume[:, :, :, 0:2, :] / (volume[:, :, :, 2:3, :] + tau)
    filtered = jnp.transpose(filtered, (1, 0, 2, 3, 4)).reshape(YWIN, NZ, 2, L)
    complex_field = lax.complex(filtered[:, :, 0, :], filtered[:, :, 1, :])
    transformed = jnp.fft.ifft(complex_field, axis=1, norm="ortho")
    return jnp.stack([jnp.real(transformed), jnp.imag(transformed)]).astype(jnp.float32)
```

```python
import functools
import math

import jax
import jax.numpy as jnp
import numpy as np
from jax import lax
from jax.experimental import pallas as pl
from jax.experimental.pallas import tpu as pltpu
from jax.sharding import PartitionSpec as P

MESH = pl.DeviceIdType.MESH
BF = jnp.bfloat16
F32 = jnp.float32
NS = 32
NG = 8
ROWS = 512
COLS = 96
NT = (((1,), (1,)), ((), ()))


def whole(n):
    return [pl.BlockSpec(memory_space=pltpu.VMEM)] * n


def pack_kernel(spec, ctf, dcol, drow, blk, pat, eye, xt, meta):
    me = lax.axis_index("slab")
    for chunk in range(12):
        plane, first = chunk // 4, chunk % 4
        src = spec[:, chunk * 256 : chunk * 256 + 256] if plane < 2 else ctf[:, first * 256 : first * 256 + 256]
        part = lax.dot_general(eye[...], src, NT, preferred_element_type=F32).astype(BF)
        for i in range(8):
            xt[first * 8 + i, plane * 32 : plane * 32 + 32, :] = part[i * 32 : i * 32 + 32, :]
    later = lax.broadcasted_iota(jnp.int32, (ROWS, ROWS), 0) < lax.broadcasted_iota(jnp.int32, (ROWS, ROWS), 1)
    same = (dcol[...] == drow[...]) & later
    pos = jnp.sum(jnp.where(same, 1.0, 0.0), axis=0, keepdims=True)
    d = drow[...]
    slot = (128 * (d >> 2) + 32 * ((d + me) & 3)).astype(F32) + pos
    code = (blk[...] * 64 + pat[...]).astype(F32)
    for t in range(4):
        meta[t : t + 1, :] = slot[:, t * 128 : t * 128 + 128]
        meta[4 + t : 5 + t, :] = code[:, t * 128 : t * 128 + 128]


def exchange_kernel(xt, meta, got, gotm, own, ownm, lsem, ssem, rsem, smsem, rmsem):
    me = lax.axis_index("slab")
    first = pltpu.make_async_copy(xt.at[me], own, lsem.at[0])
    firstm = pltpu.make_async_copy(meta, ownm, lsem.at[1])
    first.start()
    firstm.start()
    barrier = pltpu.get_barrier_semaphore()
    for t in range(1, NS):
        pl.semaphore_signal(barrier, inc=1, device_id={"slab": lax.rem(me + t, NS)}, device_id_type=MESH)
    pl.semaphore_wait(barrier, NS - 1)

    def copies(t):
        peer = lax.rem(me + t, NS)
        source = lax.rem(me + NS - t, NS)
        small = pltpu.make_async_remote_copy(
            meta, gotm.at[me], smsem.at[t], rmsem.at[t], device_id={"slab": peer}, device_id_type=MESH
        )
        big = pltpu.make_async_remote_copy(
            xt.at[peer], got.at[me], ssem.at[t], rsem.at[t], device_id={"slab": peer}, device_id_type=MESH
        )
        del source
        return small, big

    sent = [copies(t) for t in range(1, NS)]
    for small, big in sent:
        small.start()
        big.start()
    first.wait()
    firstm.wait()
    last = pltpu.make_async_copy(own, got.at[me], lsem.at[0])
    lastm = pltpu.make_async_copy(ownm, gotm.at[me], lsem.at[1])
    last.start()
    lastm.start()
    last.wait()
    lastm.wait()
    for small, big in sent:
        small.wait()
        big.wait()


def spread_kernel(got, gotm, table, iota, groups, vol, xa, pt, y, xs, st, vt):
    def pick(parts):
        lane = groups[0 : parts[0].shape[0], :] if parts[0].dtype == BF else groups[0 : parts[0].shape[0], :].astype(F32)
        return jnp.where(lane < 1.0, parts[0], jnp.where(lane < 2.0, parts[1], jnp.where(lane < 3.0, parts[2], parts[3])))

    sub = lax.broadcasted_iota(jnp.int32, (16, 128), 0)
    half = jnp.where(sub >= 8, 1.0, 0.0)

    @pl.loop(0, NS // 4)
    def _(quad):
        for jj in range(4):
            j = quad * 4 + jj
            m = gotm[j]
            xa[0:COLS, :] = got[j]
            slots = []
            for t in range(4):
                code = m[4 + t : 5 + t, :]
                blk = jnp.floor(code * (1.0 / 64.0))
                pat = code - blk * 64.0
                patb = jnp.broadcast_to(pat, (64, 128)).astype(BF)
                hot = jnp.where(patb == iota[0:64, :], 1.0, 0.0).astype(BF)
                w = jnp.dot(table[...], hot, preferred_element_type=F32)
                xa[COLS : COLS + 16, t * 128 : t * 128 + 128] = w.astype(BF)
                xa[COLS + 16 : COLS + 32, t * 128 : t * 128 + 128] = (jnp.broadcast_to(blk, (16, 128)) - half).astype(BF)
                slots.append(jnp.broadcast_to(m[t : t + 1, :], (16, 128)))
            for n in range(4):
                for t in range(4):
                    v = (slots[t] - 256.0 * n).astype(BF)
                    for g in range(16):
                        pt[g * 16 : g * 16 + 16, t * 128 : t * 128 + 128] = jnp.where(
                            v == iota[g * 16 : g * 16 + 16, :], jnp.ones_like(v), jnp.zeros_like(v)
                        )
                y[jj, :, n * 256 : n * 256 + 256] = lax.dot_general(
                    xa[...], pt[...], NT, preferred_element_type=F32
                ).astype(BF)
        lanes = pl.ds(pl.multiple_of(quad * 128, 128), 128)
        for q in range(8):
            tiles = [y[jj, :, q * 128 : q * 128 + 128] for jj in range(4)]
            for s in range(4):
                xs[q * 4 + s, :, lanes] = pick([tiles[(g - s) % 4] for g in range(4)])

    @pl.loop(0, NS // 4)
    def _(q):
        for s in range(4):
            slab = q * 4 + s
            w16 = xs[slab, COLS : COLS + 16, :]
            lab = xs[slab, COLS + 16 : COLS + 32, :]
            for i in range(32):
                u, g, b = i // 8, (i // 2) % 4, i % 2
                base = 4 * (4 * u + (g - s) % 4) + 2 * b
                st[i * 16 : i * 16 + 16, :] = jnp.where(lab == jnp.full_like(lab, base), w16, jnp.zeros_like(w16))
            for h in range(2):
                vt[s, :, h * 256 : h * 256 + 256] = lax.dot_general(
                    xs[slab, 0:COLS, :], st[h * 256 : h * 256 + 256, :], NT, preferred_element_type=F32
                )
        for u in range(4):
            tiles = [vt[s, :, u * 128 : u * 128 + 128] for s in range(4)]
            for a in range(4):
                vol[2 * u + a // 2, (a % 2) * 8 + q] = pick([tiles[(g - a) % 4] for g in range(4)])


PARTS = 4
TILES = 16 // PARTS


def reduce_kernel(v, out, local, ra, rb, lsem, sa, ka, sb, kb):
    me = lax.axis_index("grp")
    loads = []
    for i in range(NG):
        o = lax.rem(me + i, NG)
        load = pltpu.make_async_copy(v.at[o], local.at[o], lsem.at[i])
        load.start()
        loads.append(load)
    barrier = pltpu.get_barrier_semaphore()
    for step in (1, NG - 1):
        pl.semaphore_signal(barrier, inc=1, device_id={"grp": lax.rem(me + step, NG)}, device_id_type=MESH)
    pl.semaphore_wait(barrier, 2)
    for load in loads:
        load.wait()

    chains = []
    for p in range(PARTS):
        sign = 1 if p % 2 == 0 else -1
        chains.append((p, sign, 4, ra, sa, ka))
        chains.append((p, -sign, 3, rb, sb, kb))
    copies = {}

    def chunk(p, sign, hops):
        return local.at[lax.rem(me + sign * hops + NG, NG), pl.ds(p * TILES, TILES)]

    for t in range(1, 5):
        for c, (p, sign, length, buf, ssem, rsem) in enumerate(chains):
            if t > length:
                continue
            mine = chunk(p, sign, length - t + 1)
            if t == 1:
                src = mine
            else:
                copies[c, t - 1].wait_recv()
                src = buf.at[p, t - 2]
                src[...] += mine[...]
            copy = pltpu.make_async_remote_copy(
                src,
                buf.at[p, t - 1],
                ssem.at[p, t - 1],
                rsem.at[p, t - 1],
                device_id={"grp": lax.rem(me + sign + NG, NG)},
                device_id_type=MESH,
            )
            copy.start()
            copies[c, t] = copy
    for p in range(PARTS):
        copies[2 * p + 1, 3].wait_recv()
        copies[2 * p, 4].wait_recv()
        out[p * TILES : p * TILES + TILES] = local[me, p * TILES : p * TILES + TILES] + ra[p, 3] + rb[p, 2]
    for copy in copies.values():
        copy.wait_send()


def image_kernel(u, tau, are, aim, bre, bim, out, wh, wl, lhs):
    g = lax.axis_index("grp")

    @pl.loop(0, NS)
    def _(s):
        xr, xi = are[pl.ds(s, 1), :], aim[pl.ds(s, 1), :]
        rows = pl.ds(pl.multiple_of(s * 32, 32), 32)
        for part in range(2):
            w = bre[...] * xr - bim[...] * xi if part == 0 else bre[...] * xi + bim[...] * xr
            hi = w.astype(BF)
            wh[rows, part * 1024 : part * 1024 + 1024] = hi
            wl[rows, part * 1024 : part * 1024 + 1024] = (w - hi.astype(F32)).astype(BF)

    for y in range(2):
        shift = lax.rem(128 - 32 * (2 * (g & 1) + y), 128)
        for q in range(8):
            tile = u[y * 8 + q]
            scale = tile[64:96] + tau[...]
            for part in range(2):
                f = pltpu.roll(tile[part * 32 : part * 32 + 32] / scale, shift, 1)
                hi = f.astype(BF)
                r = part * 64 + y * 32
                lhs[r : r + 32, q * 128 : q * 128 + 128] = hi
                lhs[128 + r : 160 + r, q * 128 : q * 128 + 128] = (f - hi.astype(F32)).astype(BF)

    def product(first):
        cols = pl.ds(first, 256)
        full = jnp.dot(lhs[...], wh[:, cols], preferred_element_type=F32)
        return full[0:128] + full[128:256] + jnp.dot(lhs[0:128, :], wl[:, cols], preferred_element_type=F32)

    for n in range(4):
        c = product(n * 256)
        s = product(1024 + n * 256)
        out[0, :, n * 256 : n * 256 + 256] = c[0:64] - s[64:128]
        out[1, :, n * 256 : n * 256 + 256] = s[0:64] + c[64:128]


def factors():
    z = np.arange(1024)
    digit = np.arange(32)[:, None]
    coarse = 2.0 * math.pi * (32 * digit * z % 1024) / 1024
    fine = 2.0 * math.pi * (digit * z % 1024) / 1024
    scale = 1.0 / 32.0
    return [np.asarray(a, np.float32) for a in (np.cos(coarse), np.sin(coarse), scale * np.cos(fine), scale * np.sin(fine))]


def params(**more):
    return pltpu.CompilerParams(vmem_limit_bytes=60 * 1024 * 1024, **more)


def shape(dims, dtype):
    return jax.ShapeDtypeStruct(dims, dtype)


ANY = pl.BlockSpec(memory_space=pl.ANY)


def pack(spectra, ctf_sq, dest, block, pattern):
    eye = jnp.eye(256, dtype=BF)
    return pl.pallas_call(
        pack_kernel,
        out_shape=(shape((NS, COLS, ROWS), BF), shape((8, 128), F32)),
        in_specs=whole(7),
        out_specs=tuple(whole(2)),
        compiler_params=params(),
        name="pack",
    )(spectra, ctf_sq, dest, dest.reshape(1, ROWS), block.reshape(1, ROWS), pattern.reshape(1, ROWS), eye)


def exchange(xt, meta):
    dma = pltpu.SemaphoreType.DMA
    return pl.pallas_call(
        exchange_kernel,
        out_shape=(shape((NS, COLS, ROWS), BF), shape((NS, 8, 128), F32)),
        in_specs=[ANY] * 2,
        out_specs=(ANY, ANY),
        scratch_shapes=[
            pltpu.VMEM((COLS, ROWS), BF),
            pltpu.VMEM((8, 128), F32),
            dma((2,)),
            dma((NS,)),
            dma((NS,)),
            dma((NS,)),
            dma((NS,)),
        ],
        compiler_params=pltpu.CompilerParams(collective_id=0, has_side_effects=True),
        name="exchange",
    )(xt, meta)


def spread(got, gotm, pattern_table):
    iota = jnp.asarray(np.tile(np.arange(256)[:, None], (1, 128)), BF)
    groups = jnp.asarray(np.tile(np.arange(128)[None, :] // 32, (128, 1)), BF)
    table = jnp.concatenate([pattern_table.T, pattern_table.T], axis=0)
    return pl.pallas_call(
        spread_kernel,
        out_shape=shape((NG, 16, COLS, 128), F32),
        in_specs=whole(5),
        out_specs=whole(1)[0],
        scratch_shapes=[
            pltpu.VMEM((128, ROWS), BF),
            pltpu.VMEM((256, ROWS), BF),
            pltpu.VMEM((4, 128, 1024), BF),
            pltpu.VMEM((NS, 128, 1024), BF),
            pltpu.VMEM((512, 1024), BF),
            pltpu.VMEM((4, COLS, 512), F32),
        ],
        compiler_params=params(),
        name="spread",
    )(got, gotm, table, iota, groups)


def reduce_ring(vol):
    dma = pltpu.SemaphoreType.DMA
    return pl.pallas_call(
        reduce_kernel,
        out_shape=shape((16, COLS, 128), F32),
        in_specs=[ANY],
        out_specs=whole(1)[0],
        scratch_shapes=[
            pltpu.VMEM((NG, 16, COLS, 128), F32),
            pltpu.VMEM((PARTS, 4, TILES, COLS, 128), F32),
            pltpu.VMEM((PARTS, 3, TILES, COLS, 128), F32),
            dma((NG,)),
            dma((PARTS, 4)),
            dma((PARTS, 4)),
            dma((PARTS, 3)),
            dma((PARTS, 3)),
        ],
        compiler_params=params(collective_id=1, has_side_effects=True),
        name="reduce",
    )(vol)


def image_of(summed, tau):
    s = lax.axis_index("slab")
    column = lax.dynamic_slice_in_dim(tau, s * 32, 32, 0).reshape(32, 1)
    return pl.pallas_call(
        image_kernel,
        out_shape=shape((2, 64, 1024), F32),
        in_specs=whole(6),
        out_specs=whole(1)[0],
        scratch_shapes=[pltpu.VMEM((1024, 2048), BF), pltpu.VMEM((1024, 2048), BF), pltpu.VMEM((256, 1024), BF)],
        compiler_params=params(),
        name="image",
    )(summed, column, *[jnp.asarray(a) for a in factors()])


def on_device(spectra, ctf_sq, dest, block, pattern, pattern_table, tau):
    xt, meta = pack(spectra, ctf_sq, dest, block, pattern)
    got, gotm = exchange(xt, meta)
    vol = spread(got, gotm, pattern_table)
    summed = reduce_ring(vol)
    image = image_of(summed, tau)
    return jnp.transpose(image.reshape(2, 2, 32, 1024), (0, 1, 3, 2))


def solution(mesh):
    rows = P(("grp", "slab"))
    wide = P(("grp", "slab"), None)
    return jax.shard_map(
        on_device,
        mesh=mesh,
        in_specs=(wide, wide, wide, rows, rows, P(), P()),
        out_specs=P(None, "grp", None, "slab"),
        check_vma=False,
    )
```

```python
import math

import jax
import jax.numpy as jnp
import numpy as np
from jax import lax
from jax.experimental import pallas as pl
from jax.experimental.pallas import tpu as pltpu
from jax.sharding import PartitionSpec as P

MESH = pl.DeviceIdType.MESH
BF = jnp.bfloat16
F32 = jnp.float32
NS = 32
NG = 8
ROWS = 512
PIECES = 2
KX = 16
COLS = 3 * KX
NT = (((1,), (1,)), ((), ()))


def kernel(
    spec, ctf, drow, blk, pat, tau, eye, table, iota, groups, are, aim, bre, bim,
    out,
    xt0, xt1, got0, got1, meta, xa, pt, y, xs, st, vt, vol, ra, rb, wh, wl, lhs, taucol,
    ssem0, ssem1, rsem0, rsem1, sa, ka, sb, kb,
):
    me = lax.axis_index("slab")
    g = lax.axis_index("grp")
    quad0 = me // 4

    barrier = pltpu.get_barrier_semaphore()
    for t in range(1, NS):
        pl.semaphore_signal(barrier, inc=1, device_id={"slab": lax.rem(me + t, NS)}, device_id_type=MESH)
    for step in (1, NG - 1):
        pl.semaphore_signal(barrier, inc=1, device_id={"grp": lax.rem(g + step, NG)}, device_id_type=MESH)

    d = drow[...]
    dtile = [d[:, t * 128 : t * 128 + 128].astype(F32) for t in range(4)]
    dcol = [jnp.transpose(jnp.broadcast_to(v, (128, 128))) for v in dtile]
    before = lax.broadcasted_iota(jnp.int32, (128, 128), 0) < lax.broadcasted_iota(jnp.int32, (128, 128), 1)
    for t in range(4):
        pos = jnp.zeros((1, 128), F32)
        for r in range(t + 1):
            same = dcol[r] == jnp.broadcast_to(dtile[t], (128, 128))
            if r == t:
                same = same & before
            pos = pos + jnp.sum(jnp.where(same, 1.0, 0.0), axis=0, keepdims=True)
        dt = d[:, t * 128 : t * 128 + 128]
        meta[t : t + 1, :] = (dt >> 2).astype(F32)
        meta[4 + t : 5 + t, :] = (32 * ((dt + me) & 3)).astype(F32) + pos
        meta[8 + t : 9 + t, :] = blk[:, t * 128 : t * 128 + 128].astype(F32)
        meta[12 + t : 13 + t, :] = pat[:, t * 128 : t * 128 + 128].astype(F32)
    metab = meta[...].astype(BF)

    for chunk in range(12):
        plane, first = chunk // 4, chunk % 4
        src = spec[:, chunk * 256 : chunk * 256 + 256] if plane < 2 else ctf[:, first * 256 : first * 256 + 256]
        part = lax.dot_general(eye[...], src, NT, preferred_element_type=F32).astype(BF)
        for i in range(8):
            for t in range(4):
                lanes = slice(t * 128, t * 128 + 128)
                xt0[first * 8 + i, plane * 4 + t] = part[i * 32 : i * 32 + 16, lanes]
                xt1[first * 8 + i, plane * 4 + t] = part[i * 32 + 16 : i * 32 + 32, lanes]
    for s in range(NS):
        xt0[s, 12] = metab

    pl.semaphore_wait(barrier, NS - 1 + 2)
    sends = []
    for xt, got, ssem, rsem in ((xt0, got0, ssem0, rsem0), (xt1, got1, ssem1, rsem1)):
        pltpu.make_async_copy(xt.at[me], got.at[me], rsem.at[me]).start()
        for i in range(8):
            for m in range(4):
                if i == 0 and m == 0:
                    continue
                peer = lax.rem(quad0 + 8 - i, 8) * 4 + lax.rem(me + m, 4)
                copy = pltpu.make_async_remote_copy(
                    xt.at[peer], got.at[me], ssem.at[i * 4 + m], rsem.at[me],
                    device_id={"slab": peer}, device_id_type=MESH,
                )
                copy.start()
                sends.append(copy)

    @pl.loop(0, NS)
    def _(s):
        xr, xi = are[pl.ds(s, 1), :], aim[pl.ds(s, 1), :]
        rows = pl.ds(pl.multiple_of(s * 32, 32), 32)
        for part in range(2):
            w = bre[...] * xr - bim[...] * xi if part == 0 else bre[...] * xi + bim[...] * xr
            hi = w.astype(BF)
            wh[rows, part * 1024 : part * 1024 + 1024] = hi
            wl[rows, part * 1024 : part * 1024 + 1024] = (w - hi.astype(F32)).astype(BF)

    taurow = tau[:, pl.ds(pl.multiple_of(quad0 * 128, 128), 128)]
    taucol[...] = jnp.transpose(jnp.broadcast_to(taurow, (128, 128)))

    def pick(parts):
        lane = groups[0 : parts[0].shape[0], :]
        lane = lane if parts[0].dtype == BF else lane.astype(F32)
        return jnp.where(lane < 1.0, parts[0], jnp.where(lane < 2.0, parts[1], jnp.where(lane < 3.0, parts[2], parts[3])))

    sub = lax.broadcasted_iota(jnp.int32, (16, 128), 0)
    half = jnp.where(sub >= 8, 1.0, 0.0)

    def place(piece, step):
        got, rsem = ((got0, rsem0), (got1, rsem1))[piece]
        quad = lax.rem(quad0 + step, 8)
        height = COLS + 32 if piece == 0 else COLS
        for jj in range(4):
            j = quad * 4 + jj
            pltpu.make_async_copy(got.at[j], got.at[j], rsem.at[j]).wait()
            m = got0[j, 12].astype(F32)
            for t in range(4):
                lanes = slice(t * 128, t * 128 + 128)
                for plane in range(3):
                    xa[plane * 16 : plane * 16 + 16, lanes] = got[j, plane * 4 + t]
                if piece == 0:
                    patb = jnp.broadcast_to(m[12 + t : 13 + t, :], (64, 128)).astype(BF)
                    hot = jnp.where(patb == iota[0:64, :], 1.0, 0.0).astype(BF)
                    w = jnp.dot(table[...], hot, preferred_element_type=F32)
                    xa[COLS : COLS + 16, lanes] = w.astype(BF)
                    xa[COLS + 16 : COLS + 32, lanes] = (jnp.broadcast_to(m[8 + t : 9 + t, :], (16, 128)) - half).astype(BF)
            slots = [jnp.broadcast_to(m[t : t + 1, :] * 128.0 + m[4 + t : 5 + t, :], (16, 128)) for t in range(4)]
            for n in range(4):
                for t in range(4):
                    v = (slots[t] - 256.0 * n).astype(BF)
                    for r in range(16):
                        pt[r * 16 : r * 16 + 16, t * 128 : t * 128 + 128] = jnp.where(
                            v == iota[r * 16 : r * 16 + 16, :], jnp.ones_like(v), jnp.zeros_like(v)
                        )
                y[jj, 0:height, n * 256 : n * 256 + 256] = lax.dot_general(
                    xa[0:height, :], pt[...], NT, preferred_element_type=F32
                ).astype(BF)
        lanes = pl.ds(pl.multiple_of(quad * 128, 128), 128)
        for q in range(8):
            tiles = [y[jj, 0:height, q * 128 : q * 128 + 128] for jj in range(4)]
            for s in range(4):
                xs[q * 4 + s, 0:height, lanes] = pick([tiles[(l - s) % 4] for l in range(4)])

    def spread(piece, u):
        base = jnp.full((16, 1024), (16 * u).astype(F32)).astype(BF)

        @pl.loop(0, 8)
        def _(q):
            for s in range(4):
                slab = q * 4 + s
                w16 = xs[slab, COLS : COLS + 16, :]
                lab = xs[slab, COLS + 16 : COLS + 32, :] - base
                for i in range(8):
                    mine = 4 * ((i // 2 - s) % 4) + 2 * (i % 2)
                    st[s, i * 16 : i * 16 + 16, :] = jnp.where(lab == jnp.full_like(lab, mine), w16, jnp.zeros_like(w16))
                vt[s] = lax.dot_general(xs[slab, 0:COLS, :], st[s], NT, preferred_element_type=F32)
            tiles = [vt[s] for s in range(4)]
            for a in range(4):
                vol[piece, 2 * u + a // 2, (a % 2) * 8 + q] = pick([tiles[(l - a) % 4] for l in range(4)])

    ring = {}

    def hop(piece, chain, t):
        buf, ssem, rsem = ((ra, sa, ka), (rb, sb, kb))[chain]
        for part in range(2):
            sign = (1 if part == 0 else -1) * (1 if chain == 0 else -1)
            owner = lax.rem(g + sign * (4 - chain - t + 1) + NG, NG)
            mine = vol.at[piece, owner, pl.ds(part * 8, 8)]
            if t == 1:
                src = mine
            else:
                ring[piece, chain, t - 1, part].wait_recv()
                src = buf.at[piece, part, t - 2]
                src[...] += mine[...]
            copy = pltpu.make_async_remote_copy(
                src, buf.at[piece, part, t - 1], ssem.at[piece, part, t - 1], rsem.at[piece, part, t - 1],
                device_id={"grp": lax.rem(g + sign + NG, NG)}, device_id_type=MESH,
            )
            copy.start()
            ring[piece, chain, t, part] = copy

    def image(piece):
        for part in range(2):
            ring[piece, 1, 3, part].wait_recv()
            ring[piece, 0, 4, part].wait_recv()
        lam = taucol[pl.ds(pl.multiple_of(lax.rem(me, 4) * 32 + piece * KX, 16), KX), :]
        for part in range(2):
            shift = lax.rem(128 - 32 * (2 * (g & 1) + part), 128)
            for q in range(8):
                tile = vol[piece, g, part * 8 + q] + ra[piece, part, 3, q] + rb[piece, part, 2, q]
                scale = tile[2 * KX : 3 * KX] + lam
                for c in range(2):
                    f = pltpu.roll(tile[c * KX : c * KX + KX] / scale, shift, 1)
                    hi = f.astype(BF)
                    r = c * 32 + part * KX
                    lhs[r : r + KX, q * 128 : q * 128 + 128] = hi
                    lhs[64 + r : 64 + r + KX, q * 128 : q * 128 + 128] = (f - hi.astype(F32)).astype(BF)

        def product(first):
            cols = slice(first, first + 256)
            full = jnp.dot(lhs[...], wh[:, cols], preferred_element_type=F32)
            return full[0:64] + full[64:128] + jnp.dot(lhs[0:64, :], wl[:, cols], preferred_element_type=F32)

        for n in range(4):
            c = product(n * 256)
            s = product(1024 + n * 256)
            for part in range(2):
                rows = slice(part * 32 + piece * KX, part * 32 + piece * KX + KX)
                low, high = slice(part * KX, part * KX + KX), slice(32 + part * KX, 32 + part * KX + KX)
                out[0, rows, n * 256 : n * 256 + 256] = c[low] - s[high]
                out[1, rows, n * 256 : n * 256 + 256] = s[low] + c[high]

    far = lax.rem(g + 4, NG) // 2
    way = 1 - 2 * (g & 1)
    order = [far, lax.rem(far - way + 4, 4), lax.rem(far + way + 4, 4), g // 2]

    @pl.loop(0, 8)
    def _(step):
        place(0, step)

    spread(0, order[0])
    hop(0, 0, 1)
    spread(0, order[1])
    hop(0, 1, 1)
    spread(0, order[2])
    hop(0, 0, 2)
    spread(0, order[3])
    hop(0, 1, 2)

    def places(first, last):
        @pl.loop(first, last)
        def _(step):
            place(1, step)

    places(0, 2)
    hop(0, 0, 3)
    places(2, 4)
    hop(0, 1, 3)
    places(4, 6)
    hop(0, 0, 4)
    places(6, 8)
    spread(1, order[0])
    hop(1, 0, 1)
    spread(1, order[1])
    hop(1, 1, 1)
    spread(1, order[2])
    hop(1, 0, 2)
    spread(1, order[3])
    hop(1, 1, 2)
    hop(1, 0, 3)
    image(0)
    hop(1, 1, 3)
    hop(1, 0, 4)
    image(1)
    for copy in sends:
        copy.wait_send()
    for copy in ring.values():
        copy.wait_send()


def factors():
    z = np.arange(1024)
    digit = np.arange(32)[:, None]
    coarse = 2.0 * math.pi * (32 * digit * z % 1024) / 1024
    fine = 2.0 * math.pi * (digit * z % 1024) / 1024
    scale = 1.0 / 32.0
    return [np.asarray(a, np.float32) for a in (np.cos(coarse), np.sin(coarse), scale * np.cos(fine), scale * np.sin(fine))]


def on_device(spectra, ctf_sq, dest, block, pattern, pattern_table, tau):
    iota = jnp.asarray(np.tile(np.arange(256)[:, None], (1, 128)), BF)
    groups = jnp.asarray(np.tile(np.arange(128)[None, :] // 32, (128, 1)), BF)
    table = jnp.concatenate([pattern_table.T, pattern_table.T], axis=0)
    dma = pltpu.SemaphoreType.DMA
    operands = (
        spectra, ctf_sq, dest.reshape(1, ROWS), block.reshape(1, ROWS), pattern.reshape(1, ROWS), tau.reshape(1, 1024),
        jnp.eye(256, dtype=BF), table, iota, groups, *[jnp.asarray(a) for a in factors()],
    )
    image = pl.pallas_call(
        kernel,
        out_shape=jax.ShapeDtypeStruct((2, 64, 1024), F32),
        in_specs=[pl.BlockSpec(memory_space=pltpu.VMEM)] * len(operands),
        out_specs=pl.BlockSpec(memory_space=pltpu.VMEM),
        scratch_shapes=[
            pltpu.VMEM((NS, 13, 16, 128), BF),
            pltpu.VMEM((NS, 12, 16, 128), BF),
            pltpu.VMEM((NS, 13, 16, 128), BF),
            pltpu.VMEM((NS, 12, 16, 128), BF),
            pltpu.VMEM((16, 128), F32),
            pltpu.VMEM((COLS + 32, ROWS), BF),
            pltpu.VMEM((256, ROWS), BF),
            pltpu.VMEM((4, COLS + 32, 1024), BF),
            pltpu.VMEM((NS, COLS + 32, 1024), BF),
            pltpu.VMEM((4, 128, 1024), BF),
            pltpu.VMEM((4, COLS, 128), F32),
            pltpu.VMEM((PIECES, NG, 16, COLS, 128), F32),
            pltpu.VMEM((PIECES, 2, 4, 8, COLS, 128), F32),
            pltpu.VMEM((PIECES, 2, 3, 8, COLS, 128), F32),
            pltpu.VMEM((1024, 2048), BF),
            pltpu.VMEM((1024, 2048), BF),
            pltpu.VMEM((128, 1024), BF),
            pltpu.VMEM((128, 128), F32),
            dma((NS,)),
            dma((NS,)),
            dma((NS,)),
            dma((NS,)),
            dma((PIECES, 2, 4)),
            dma((PIECES, 2, 4)),
            dma((PIECES, 2, 3)),
            dma((PIECES, 2, 3)),
        ],
        compiler_params=pltpu.CompilerParams(
            collective_id=0, has_side_effects=True, vmem_limit_bytes=62 * 1024 * 1024
        ),
        name="backproject",
    )(*operands)
    return jnp.transpose(image.reshape(2, 2, 32, 1024), (0, 1, 3, 2))


def solution(mesh):
    rows = P(("grp", "slab"))
    wide = P(("grp", "slab"), None)
    return jax.shard_map(
        on_device,
        mesh=mesh,
        in_specs=(wide, wide, wide, rows, rows, P(), P()),
        out_specs=P(None, "grp", None, "slab"),
        check_vma=False,
    )
```

```python
import math

import jax
import jax.numpy as jnp
import numpy as np
from jax import lax
from jax.experimental import pallas as pl
from jax.experimental.pallas import tpu as pltpu
from jax.sharding import PartitionSpec as P

MESH = pl.DeviceIdType.MESH
BF = jnp.bfloat16
F32 = jnp.float32
NS = 32
NG = 8
ROWS = 512
PIECES = 2
KX = 16
SMALL = 11
COLS = 3 * KX
NT = (((1,), (1,)), ((), ()))


ROW_STEPS = (1, 3, 0, 2)


def steps_away(step):
    late, r = step // 4, step % 4
    t = (r + r // 2) % 2
    even, odd = 2 * (r % 2), 2 * (r % 2) + 1
    return (even, (1 - late) * (1 + 2 * t) + late * (2 - 2 * t)), (odd, (1 - late) * (3 - 2 * t) + late * 2 * t)


def kernel(
    spec, ctf, *rest,
):
    small_in, out = rest[:SMALL], rest[SMALL]
    raw, small = rest[SMALL + 1], rest[SMALL + 2 : 2 * SMALL + 2]
    (
        xt0, xt1, got0, got1, mrow, perm, meta, xa, pt, y, xs0, xs1, st, vt, vol, ra, rb, wh, wl, lhs, taucol,
        insem, smallsem, ssem0, ssem1, rsem0, rsem1, sa, ka, sb, kb,
    ) = rest[2 * SMALL + 2 :]
    drow, blk, pat, tau, iota, tab, groups, are, aim, bre, bim = small
    me = lax.axis_index("slab")
    g = lax.axis_index("grp")
    row, col, core = me // 8, (me // 2) % 4, me % 2

    barrier = pltpu.get_barrier_semaphore()
    for t in range(1, NS):
        pl.semaphore_signal(barrier, inc=1, device_id={"slab": lax.rem(me + t, NS)}, device_id_type=MESH)
    for step in (1, NG - 1):
        pl.semaphore_signal(barrier, inc=1, device_id={"grp": lax.rem(g + step, NG)}, device_id_type=MESH)

    loads = [pltpu.make_async_copy(a, b, smallsem.at[i]) for i, (a, b) in enumerate(zip(small_in, small))]
    for load in loads[:8]:
        load.start()
    fetches = []
    for i in range(4):
        first = lax.rem(row + 4 - ROW_STEPS[i], 4) * 256
        for plane in range(3):
            source, start = (spec, first + plane * 1024) if plane < 2 else (ctf, first)
            fetch = pltpu.make_async_copy(
                source.at[:, pl.ds(pl.multiple_of(start, 256), 256)], raw.at[i, plane], insem.at[i, plane]
            )
            fetch.start()
            fetches.append(fetch)
    for load in loads[8:]:
        load.start()
    for load in loads[:8]:
        load.wait()

    d = drow[...]
    dtile = [d[:, t * 128 : t * 128 + 128].astype(F32) for t in range(4)]
    dcol = [jnp.transpose(jnp.broadcast_to(v, (128, 128))) for v in dtile]
    before = lax.broadcasted_iota(jnp.int32, (128, 128), 0) < lax.broadcasted_iota(jnp.int32, (128, 128), 1)
    mrow[...] = jnp.zeros_like(mrow)
    for t in range(4):
        lanes = slice(t * 128, t * 128 + 128)
        pos = jnp.zeros((1, 128), F32)
        rank = jnp.zeros((1, 128), F32)
        wide = jnp.broadcast_to(dtile[t], (128, 128))
        for r in range(4):
            rank = rank + jnp.sum(jnp.where(dcol[r] < wide, 1.0, 0.0), axis=0, keepdims=True)
            if r <= t:
                same = dcol[r] == wide
                if r == t:
                    same = same & before
                pos = pos + jnp.sum(jnp.where(same, 1.0, 0.0), axis=0, keepdims=True)
        dt = d[:, lanes]
        mrow[0:1, lanes] = (dt >> 2).astype(F32)
        mrow[1:2, lanes] = (32 * ((dt + me) & 3)).astype(F32) + pos
        mrow[2:3, lanes] = blk[:, lanes].astype(F32)
        mrow[3:4, lanes] = pat[:, lanes].astype(F32)
        rank16 = jnp.broadcast_to(rank + pos, (16, 128))
        for n in range(2):
            v = (rank16 - 256.0 * n).astype(BF)
            for r in range(16):
                perm[n * 256 + r * 16 : n * 256 + r * 16 + 16, lanes] = jnp.where(
                    v == iota[r * 16 : r * 16 + 16, :], jnp.ones_like(v), jnp.zeros_like(v)
                )
    mrow[...] = lax.dot_general(mrow[...].astype(BF), perm[...], NT, preferred_element_type=F32)
    for v in range(4):
        for t in range(4):
            meta[v * 4 + t : v * 4 + t + 1, :] = mrow[v : v + 1, t * 128 : t * 128 + 128]
    metab = meta[...].astype(BF)

    sends = []

    def send(piece, step):
        xt, got, ssem, rsem = ((xt0, got0, ssem0, rsem0), (xt1, got1, ssem1, rsem1))[piece]
        for odd, (dx, dy) in enumerate(steps_away(step)):
            chip = lax.rem(row + 4 - dy, 4) * 4 + lax.rem(col + 4 - dx, 4)
            for m in range(2):
                if dx or dy or m:
                    copy = pltpu.make_async_remote_copy(
                        xt.at[chip * 2 + lax.rem(core + m, 2)], got.at[me], ssem.at[step * 4 + odd * 2 + m], rsem.at[me],
                        device_id={"slab": chip * 2 + lax.rem(core + m, 2)}, device_id_type=MESH,
                    )
                    copy.start()
                    sends.append(copy)

    for i in range(4):
        octet = lax.rem(row + 4 - ROW_STEPS[i], 4) * 8
        for plane in range(3):
            fetches[i * 3 + plane].wait()
            part = lax.dot_general(
                jnp.transpose(raw[i, plane]), perm[...], NT, preferred_element_type=F32
            ).astype(BF)
            for k in range(8):
                for t in range(4):
                    lanes = slice(t * 128, t * 128 + 128)
                    xt0[octet + k, plane * 4 + t] = part[k * 32 : k * 32 + 16, lanes]
                    xt1[octet + k, plane * 4 + t] = part[k * 32 + 16 : k * 32 + 32, lanes]
        for k in range(8):
            xt0[octet + k, 12] = metab
        if i == 1:
            pl.semaphore_wait(barrier, NS - 1 + 2)
            for step in range(4):
                send(0, step)
        if i == 2:
            pltpu.make_async_copy(xt0.at[me], got0.at[me], rsem0.at[me]).start()
            pltpu.make_async_copy(xt1.at[me], got1.at[me], rsem1.at[me]).start()
    for step in range(4, 8):
        send(0, step)
    tabf = tab[...].astype(F32)
    table = jnp.concatenate([tabf, tabf], axis=0).astype(BF)

    def tables():
        for load in loads[8:]:
            load.wait()

        @pl.loop(0, NS)
        def _(s):
            xr, xi = are[pl.ds(s, 1), :], aim[pl.ds(s, 1), :]
            rows = pl.ds(pl.multiple_of(s * 32, 32), 32)
            for part in range(2):
                w = bre[...] * xr - bim[...] * xi if part == 0 else bre[...] * xi + bim[...] * xr
                hi = w.astype(BF)
                wh[rows, part * 1024 : part * 1024 + 1024] = hi
                wl[rows, part * 1024 : part * 1024 + 1024] = (w - hi.astype(F32)).astype(BF)

        taurow = tau[:, pl.ds(pl.multiple_of(me // 4 * 128, 128), 128)]
        taucol[...] = jnp.transpose(jnp.broadcast_to(taurow, (128, 128)))

    def pick(parts):
        lane = groups[0 : parts[0].shape[0], :]
        lane = lane if parts[0].dtype == BF else lane.astype(F32)
        return jnp.where(lane < 1.0, parts[0], jnp.where(lane < 2.0, parts[1], jnp.where(lane < 3.0, parts[2], parts[3])))

    sub = lax.broadcasted_iota(jnp.int32, (16, 128), 0)
    half = jnp.where(sub >= 8, 1.0, 0.0)

    def place(piece, step):
        got, rsem = ((got0, rsem0), (got1, rsem1))[piece]
        even, odd = steps_away(step)
        height = COLS + 32 if piece == 0 else COLS
        for jj in range(4):
            same = 1 - lax.rem(col + jj // 2, 2)
            dx, dy = (same * e + (1 - same) * o for e, o in zip(even, odd))
            j = (lax.rem(row + dy, 4) * 4 + lax.rem(col + dx, 4)) * 2 + jj % 2
            pltpu.make_async_copy(got.at[j], got.at[j], rsem.at[j]).wait()
            m = got0[j, 12].astype(F32)
            for t in range(4):
                lanes = slice(t * 128, t * 128 + 128)
                for plane in range(3):
                    xa[plane * 16 : plane * 16 + 16, lanes] = got[j, plane * 4 + t]
                if piece == 0:
                    patb = jnp.broadcast_to(m[12 + t : 13 + t, :], (64, 128)).astype(BF)
                    hot = jnp.where(patb == iota[0:64, :], 1.0, 0.0).astype(BF)
                    w = jnp.dot(table, hot, preferred_element_type=F32)
                    xa[COLS : COLS + 16, lanes] = w.astype(BF)
                    xa[COLS + 16 : COLS + 32, lanes] = (jnp.broadcast_to(m[8 + t : 9 + t, :], (16, 128)) - half).astype(BF)
            slots = [jnp.broadcast_to(m[t : t + 1, :] * 128.0 + m[4 + t : 5 + t, :], (16, 128)) for t in range(4)]
            low, high = (0, 0, 0, 2), (2, 4, 4, 4)
            for n in range(4):
                band = slice(low[n] * 128, high[n] * 128)
                for t in range(low[n], high[n]):
                    v = (slots[t] - 256.0 * n).astype(BF)
                    for r in range(16):
                        pt[n % 2, r * 16 : r * 16 + 16, t * 128 : t * 128 + 128] = jnp.where(
                            v == iota[r * 16 : r * 16 + 16, :], jnp.ones_like(v), jnp.zeros_like(v)
                        )
                y[jj, 0:height, n * 256 : n * 256 + 256] = lax.dot_general(
                    xa[0:height, band], pt[n % 2, :, band], NT, preferred_element_type=F32
                ).astype(BF)
        xs = xs0 if piece == 0 else xs1
        lanes = pl.ds(pl.multiple_of(step * 128, 128), 128)
        for q in range(8):
            tiles = [y[jj, 0:height, q * 128 : q * 128 + 128] for jj in range(4)]
            for s in range(4):
                xs[q * 4 + s, 0:height, lanes] = pick([tiles[(l - s) % 4] for l in range(4)])

    def spread(piece, groups_of):
        width = 128 * len(groups_of)
        xs = xs0 if piece == 0 else xs1
        shifts = [[jnp.full((16, 1024), (8 * o).astype(F32)).astype(BF) for o in owners] for owners in groups_of]

        @pl.loop(0, 8)
        def _(q):
            for s in range(4):
                slab = q * 4 + s
                w16 = xs0[slab, COLS : COLS + 16, :]
                lab16 = xs0[slab, COLS + 16 : COLS + 32, :]
                for n, shift in enumerate(shifts):
                    lab = [lab16 - shift[0], lab16 - shift[1]]
                    for i in range(8):
                        a = (i // 2 - s) % 4
                        mine = 4 * (a % 2) + 2 * (i % 2)
                        st[s, n * 128 + i * 16 : n * 128 + i * 16 + 16, :] = jnp.where(
                            lab[a // 2] == jnp.full_like(w16, mine), w16, jnp.zeros_like(w16)
                        )
                vt[s, :, 0:width] = lax.dot_general(xs[slab, 0:COLS, :], st[s, 0:width, :], NT, preferred_element_type=F32)
            for n, owners in enumerate(groups_of):
                tiles = [vt[s, :, n * 128 : n * 128 + 128] for s in range(4)]
                for a in range(4):
                    vol[piece, owners[a // 2], (a % 2) * 8 + q] = pick([tiles[(l - a) % 4] for l in range(4)])

    ring = {}

    def hop(piece, chain, t, parts=(0, 1)):
        buf, ssem, rsem = ((ra, sa, ka), (rb, sb, kb))[chain]
        for part in parts:
            sign = (1 if part == 0 else -1) * (1 if chain == 0 else -1)
            owner = lax.rem(g + sign * (4 - chain - t + 1) + NG, NG)
            mine = vol.at[piece, owner, pl.ds(part * 8, 8)]
            if t == 1:
                src = mine
            else:
                ring[piece, chain, t - 1, part].wait_recv()
                src = buf.at[piece, part, t - 2]
                src[...] += mine[...]
            copy = pltpu.make_async_remote_copy(
                src, buf.at[piece, part, t - 1], ssem.at[piece, part, t - 1], rsem.at[piece, part, t - 1],
                device_id={"grp": lax.rem(g + sign + NG, NG)}, device_id_type=MESH,
            )
            copy.start()
            ring[piece, chain, t, part] = copy

    def image(piece):
        for part in range(2):
            ring[piece, 1, 3, part].wait_recv()
            ring[piece, 0, 4, part].wait_recv()
        lam = taucol[pl.ds(pl.multiple_of(lax.rem(me, 4) * 32 + piece * KX, 16), KX), :]
        for part in range(2):
            shift = lax.rem(128 - 32 * (2 * (g & 1) + part), 128)
            for q in range(8):
                tile = vol[piece, g, part * 8 + q] + ra[piece, part, 3, q] + rb[piece, part, 2, q]
                scale = tile[2 * KX : 3 * KX] + lam
                for c in range(2):
                    f = pltpu.roll(tile[c * KX : c * KX + KX] / scale, shift, 1)
                    hi = f.astype(BF)
                    r = c * 32 + part * KX
                    lhs[r : r + KX, q * 128 : q * 128 + 128] = hi
                    lhs[64 + r : 64 + r + KX, q * 128 : q * 128 + 128] = (f - hi.astype(F32)).astype(BF)

        def product(first):
            cols = slice(first, first + 256)
            full = jnp.dot(lhs[...], wh[:, cols], preferred_element_type=F32)
            return full[0:64] + full[64:128] + jnp.dot(lhs[0:64, :], wl[:, cols], preferred_element_type=F32)

        for n in range(4):
            c = product(n * 256)
            s = product(1024 + n * 256)
            for part in range(2):
                rows = slice(part * 32 + piece * KX, part * 32 + piece * KX + KX)
                low, high = slice(part * KX, part * KX + KX), slice(32 + part * KX, 32 + part * KX + KX)
                out[0, rows, n * 256 : n * 256 + 256] = c[low] - s[high]
                out[1, rows, n * 256 : n * 256 + 256] = s[low] + c[high]

    def owners(i, j):
        first, second = lax.rem(g + i, NG), lax.rem(g + j, NG)
        odd = first & 1
        return (first + odd * (second - first), second + odd * (first - second))

    pairs = [owners(4, 3), owners(5, 2), owners(6, 1), owners(7, 0)]

    def places(piece, first, last):
        @pl.loop(first, last)
        def _(step):
            place(piece, step)

    places(0, 0, 4)
    for step in range(4):
        send(1, step)
    places(0, 4, 6)
    for step in range(4, 6):
        send(1, step)
    places(0, 6, 8)
    for step in range(6, 8):
        send(1, step)
    spread(0, pairs[0:1])
    hop(0, 0, 1)
    hop(0, 1, 1, (1,))
    spread(0, pairs[1:2])
    hop(0, 1, 1, (0,))
    places(1, 0, 2)
    hop(0, 0, 2)
    spread(0, pairs[2:3])
    hop(0, 1, 2)
    spread(0, pairs[3:4])
    hop(0, 0, 3)
    places(1, 2, 4)
    hop(0, 1, 3)
    places(1, 4, 6)
    hop(0, 0, 4)
    places(1, 6, 8)
    spread(1, pairs[0:1])
    hop(1, 0, 1)
    hop(1, 1, 1, (1,))
    spread(1, pairs[1:2])
    hop(1, 1, 1, (0,))
    hop(1, 0, 2)
    spread(1, pairs[2:3])
    hop(1, 1, 2)
    spread(1, pairs[3:4])
    hop(1, 0, 3)
    tables()
    hop(1, 1, 3)
    image(0)
    hop(1, 0, 4)
    image(1)
    for copy in sends:
        copy.wait_send()
    for copy in ring.values():
        copy.wait_send()


def factors():
    z = np.arange(1024)
    digit = np.arange(32)[:, None]
    coarse = 2.0 * math.pi * (32 * digit * z % 1024) / 1024
    fine = 2.0 * math.pi * (digit * z % 1024) / 1024
    scale = 1.0 / 32.0
    return [np.asarray(a, np.float32) for a in (np.cos(coarse), np.sin(coarse), scale * np.cos(fine), scale * np.sin(fine))]


def on_device(spectra, ctf_sq, dest, block, pattern, pattern_table, tau):
    iota = jnp.asarray(np.tile(np.arange(256)[:, None], (1, 128)), BF)
    groups = jnp.asarray(np.tile(np.arange(128)[None, :] // 32, (128, 1)), BF)
    dma = pltpu.SemaphoreType.DMA
    small = (
        dest.reshape(1, ROWS), block.reshape(1, ROWS), pattern.reshape(1, ROWS), tau.reshape(1, 1024),
        iota, pattern_table.T, groups, *[jnp.asarray(a) for a in factors()],
    )
    operands = (spectra, ctf_sq, *small)
    image = pl.pallas_call(
        kernel,
        out_shape=jax.ShapeDtypeStruct((2, 64, 1024), F32),
        in_specs=[pl.BlockSpec(memory_space=pl.ANY)] * len(operands),
        out_specs=pl.BlockSpec(memory_space=pltpu.VMEM),
        scratch_shapes=[
            pltpu.VMEM((4, 3, ROWS, 256), BF),
            *[pltpu.VMEM(a.shape, a.dtype) for a in small],
            pltpu.VMEM((NS, 13, 16, 128), BF),
            pltpu.VMEM((NS, 12, 16, 128), BF),
            pltpu.VMEM((NS, 13, 16, 128), BF),
            pltpu.VMEM((NS, 12, 16, 128), BF),
            pltpu.VMEM((16, ROWS), F32),
            pltpu.VMEM((ROWS, ROWS), BF),
            pltpu.VMEM((16, 128), F32),
            pltpu.VMEM((COLS + 32, ROWS), BF),
            pltpu.VMEM((2, 256, ROWS), BF),
            pltpu.VMEM((4, COLS + 32, 1024), BF),
            pltpu.VMEM((NS, COLS + 32, 1024), BF),
            pltpu.VMEM((NS, COLS, 1024), BF),
            pltpu.VMEM((4, 256, 1024), BF),
            pltpu.VMEM((4, COLS, 256), F32),
            pltpu.VMEM((PIECES, NG, 16, COLS, 128), F32),
            pltpu.VMEM((PIECES, 2, 4, 8, COLS, 128), F32),
            pltpu.VMEM((PIECES, 2, 3, 8, COLS, 128), F32),
            pltpu.VMEM((1024, 2048), BF),
            pltpu.VMEM((1024, 2048), BF),
            pltpu.VMEM((128, 1024), BF),
            pltpu.VMEM((128, 128), F32),
            dma((4, 3)),
            dma((SMALL,)),
            dma((NS,)),
            dma((NS,)),
            dma((NS,)),
            dma((NS,)),
            dma((PIECES, 2, 4)),
            dma((PIECES, 2, 4)),
            dma((PIECES, 2, 3)),
            dma((PIECES, 2, 3)),
        ],
        compiler_params=pltpu.CompilerParams(
            collective_id=0, has_side_effects=True, vmem_limit_bytes=62 * 1024 * 1024
        ),
        name="backproject",
    )(*operands)
    return jnp.transpose(image.reshape(2, 2, 32, 1024), (0, 1, 3, 2))


def solution(mesh):
    rows = P(("grp", "slab"))
    wide = P(("grp", "slab"), None)
    return jax.shard_map(
        on_device,
        mesh=mesh,
        in_specs=(wide, wide, wide, rows, rows, P(), P()),
        out_specs=P(None, "grp", None, "slab"),
        check_vma=False,
    )
```

```python
import math

import jax
import jax.numpy as jnp
import numpy as np
from jax import lax
from jax.experimental import pallas as pl
from jax.experimental.pallas import tpu as pltpu
from jax.sharding import PartitionSpec as P

MESH = pl.DeviceIdType.MESH
BF = jnp.bfloat16
F32 = jnp.float32
NS = 32
NG = 8
ROWS = 512
PIECES = 2
KX = 16
SMALL = 11
COLS = 3 * KX
NT = (((1,), (1,)), ((), ()))


ROW_STEPS = (1, 3, 0, 2)


def steps_away(step):
    late, r = step // 4, step % 4
    t = (r + r // 2) % 2
    even, odd = 2 * (r % 2), 2 * (r % 2) + 1
    return (even, (1 - late) * (1 + 2 * t) + late * (2 - 2 * t)), (odd, (1 - late) * (3 - 2 * t) + late * 2 * t)


def kernel(
    spec, ctf, *rest,
):
    small_in, out = rest[:SMALL], rest[SMALL]
    raw, small = rest[SMALL + 1], rest[SMALL + 2 : 2 * SMALL + 2]
    (
        xt0, xt1, got0, got1, mrow, perm, meta, xa, pt, y, xs0, xs1, st, vt, vol, ra, rb, wh, wl, lhs, taucol,
        insem, smallsem, ssem0, ssem1, rsem0, rsem1, sa, ka, sb, kb,
    ) = rest[2 * SMALL + 2 :]
    drow, blk, pat, tau, iota, tab, groups, are, aim, bre, bim = small
    me = lax.axis_index("slab")
    g = lax.axis_index("grp")
    row, col, core = me // 8, (me // 2) % 4, me % 2

    barrier = pltpu.get_barrier_semaphore()
    for t in range(1, NS):
        pl.semaphore_signal(barrier, inc=1, device_id={"slab": lax.rem(me + t, NS)}, device_id_type=MESH)
    for step in (1, NG - 1):
        pl.semaphore_signal(barrier, inc=1, device_id={"grp": lax.rem(g + step, NG)}, device_id_type=MESH)

    loads = [pltpu.make_async_copy(a, b, smallsem.at[i]) for i, (a, b) in enumerate(zip(small_in, small))]
    for load in loads[:8]:
        load.start()
    fetches = []
    for i in range(4):
        first = lax.rem(row + 4 - ROW_STEPS[i], 4) * 256
        for plane in range(3):
            source, start = (spec, first + plane * 1024) if plane < 2 else (ctf, first)
            fetch = pltpu.make_async_copy(
                source.at[:, pl.ds(pl.multiple_of(start, 256), 256)], raw.at[i, plane], insem.at[i, plane]
            )
            fetch.start()
            fetches.append(fetch)
    for load in loads[8:]:
        load.start()
    for load in loads[:8]:
        load.wait()

    d = drow[...]
    dtile = [d[:, t * 128 : t * 128 + 128].astype(F32) for t in range(4)]
    dcol = [jnp.transpose(jnp.broadcast_to(v, (128, 128))) for v in dtile]
    before = lax.broadcasted_iota(jnp.int32, (128, 128), 0) < lax.broadcasted_iota(jnp.int32, (128, 128), 1)
    mrow[...] = jnp.zeros_like(mrow)
    for t in range(4):
        lanes = slice(t * 128, t * 128 + 128)
        pos = jnp.zeros((1, 128), F32)
        rank = jnp.zeros((1, 128), F32)
        wide = jnp.broadcast_to(dtile[t], (128, 128))
        for r in range(4):
            rank = rank + jnp.sum(jnp.where(dcol[r] < wide, 1.0, 0.0), axis=0, keepdims=True)
            if r <= t:
                same = dcol[r] == wide
                if r == t:
                    same = same & before
                pos = pos + jnp.sum(jnp.where(same, 1.0, 0.0), axis=0, keepdims=True)
        dt = d[:, lanes]
        mrow[0:1, lanes] = (dt >> 2).astype(F32)
        mrow[1:2, lanes] = (32 * ((dt + me) & 3)).astype(F32) + pos
        mrow[2:3, lanes] = blk[:, lanes].astype(F32)
        mrow[3:4, lanes] = pat[:, lanes].astype(F32)
        rank16 = jnp.broadcast_to(rank + pos, (16, 128))
        for n in range(2):
            v = (rank16 - 256.0 * n).astype(BF)
            for r in range(16):
                perm[n * 256 + r * 16 : n * 256 + r * 16 + 16, lanes] = jnp.where(
                    v == iota[r * 16 : r * 16 + 16, :], jnp.ones_like(v), jnp.zeros_like(v)
                )
    mrow[...] = lax.dot_general(mrow[...].astype(BF), perm[...], NT, preferred_element_type=F32)
    for v in range(4):
        for t in range(4):
            meta[v * 4 + t : v * 4 + t + 1, :] = mrow[v : v + 1, t * 128 : t * 128 + 128]
    metab = meta[...].astype(BF)

    sends = []

    def send(piece, step):
        xt, got, ssem, rsem = ((xt0, got0, ssem0, rsem0), (xt1, got1, ssem1, rsem1))[piece]
        for odd, (dx, dy) in enumerate(steps_away(step)):
            chip = lax.rem(row + 4 - dy, 4) * 4 + lax.rem(col + 4 - dx, 4)
            for m in range(2):
                if dx or dy or m:
                    copy = pltpu.make_async_remote_copy(
                        xt.at[chip * 2 + lax.rem(core + m, 2)], got.at[me], ssem.at[step * 4 + odd * 2 + m], rsem.at[me],
                        device_id={"slab": chip * 2 + lax.rem(core + m, 2)}, device_id_type=MESH,
                    )
                    copy.start()
                    sends.append(copy)

    for i in range(4):
        octet = lax.rem(row + 4 - ROW_STEPS[i], 4) * 8
        for plane in range(3):
            fetches[i * 3 + plane].wait()
            part = lax.dot_general(
                jnp.transpose(raw[i, plane]), perm[...], NT, preferred_element_type=F32
            ).astype(BF)
            for k in range(8):
                for t in range(4):
                    lanes = slice(t * 128, t * 128 + 128)
                    xt0[octet + k, plane * 4 + t] = part[k * 32 : k * 32 + 16, lanes]
                    xt1[octet + k, plane * 4 + t] = part[k * 32 + 16 : k * 32 + 32, lanes]
        for k in range(8):
            xt0[octet + k, 12] = metab
        if i == 1:
            pl.semaphore_wait(barrier, NS - 1 + 2)
            for step in range(4):
                send(0, step)
        if i == 2:
            pltpu.make_async_copy(xt0.at[me], got0.at[me], rsem0.at[me]).start()
            pltpu.make_async_copy(xt1.at[me], got1.at[me], rsem1.at[me]).start()
    for step in range(4, 8):
        send(0, step)
    tabf = tab[...].astype(F32)
    table = jnp.concatenate([tabf, tabf], axis=0).astype(BF)

    def tables():
        for load in loads[8:]:
            load.wait()

        @pl.loop(0, NS)
        def _(s):
            xr, xi = are[pl.ds(s, 1), :], aim[pl.ds(s, 1), :]
            rows = pl.ds(pl.multiple_of(s * 32, 32), 32)
            for part in range(2):
                w = bre[...] * xr - bim[...] * xi if part == 0 else bre[...] * xi + bim[...] * xr
                hi = w.astype(BF)
                wh[rows, part * 1024 : part * 1024 + 1024] = hi
                wl[rows, part * 1024 : part * 1024 + 1024] = (w - hi.astype(F32)).astype(BF)

        taurow = tau[:, pl.ds(pl.multiple_of(me // 4 * 128, 128), 128)]
        taucol[...] = jnp.transpose(jnp.broadcast_to(taurow, (128, 128)))

    def pick(parts):
        lane = groups[0 : parts[0].shape[0], :]
        lane = lane if parts[0].dtype == BF else lane.astype(F32)
        return jnp.where(lane < 1.0, parts[0], jnp.where(lane < 2.0, parts[1], jnp.where(lane < 3.0, parts[2], parts[3])))

    sub = lax.broadcasted_iota(jnp.int32, (16, 128), 0)
    half = jnp.where(sub >= 8, 1.0, 0.0)

    def place(piece, step):
        got, rsem = ((got0, rsem0), (got1, rsem1))[piece]
        even, odd = steps_away(step)
        height = COLS + 32 if piece == 0 else COLS
        sources = []
        for jj in range(4):
            same = 1 - lax.rem(col + jj // 2, 2)
            dx, dy = (same * e + (1 - same) * o for e, o in zip(even, odd))
            j = (lax.rem(row + dy, 4) * 4 + lax.rem(col + dx, 4)) * 2 + jj % 2
            pltpu.make_async_copy(got.at[j], got.at[j], rsem.at[j]).wait()
            sources.append(j)
        for jj, j in enumerate(sources):
            m = got0[j, 12].astype(F32)
            for t in range(4):
                lanes = slice(t * 128, t * 128 + 128)
                for plane in range(3):
                    xa[plane * 16 : plane * 16 + 16, lanes] = got[j, plane * 4 + t]
                if piece == 0:
                    patb = jnp.broadcast_to(m[12 + t : 13 + t, :], (64, 128)).astype(BF)
                    hot = jnp.where(patb == iota[0:64, :], 1.0, 0.0).astype(BF)
                    w = jnp.dot(table, hot, preferred_element_type=F32)
                    xa[COLS : COLS + 16, lanes] = w.astype(BF)
                    xa[COLS + 16 : COLS + 32, lanes] = (jnp.broadcast_to(m[8 + t : 9 + t, :], (16, 128)) - half).astype(BF)
            slots = [jnp.broadcast_to(m[t : t + 1, :] * 128.0 + m[4 + t : 5 + t, :], (16, 128)) for t in range(4)]
            low, high = (0, 0, 0, 2), (2, 4, 4, 4)
            for n in range(4):
                band = slice(low[n] * 128, high[n] * 128)
                for t in range(low[n], high[n]):
                    v = (slots[t] - 256.0 * n).astype(BF)
                    for r in range(16):
                        pt[n % 2, r * 16 : r * 16 + 16, t * 128 : t * 128 + 128] = jnp.where(
                            v == iota[r * 16 : r * 16 + 16, :], jnp.ones_like(v), jnp.zeros_like(v)
                        )
                y[jj, 0:height, n * 256 : n * 256 + 256] = lax.dot_general(
                    xa[0:height, band], pt[n % 2, :, band], NT, preferred_element_type=F32
                ).astype(BF)
        xs = xs0 if piece == 0 else xs1
        lanes = pl.ds(pl.multiple_of(step * 128, 128), 128)
        for q in range(8):
            tiles = [y[jj, 0:height, q * 128 : q * 128 + 128] for jj in range(4)]
            for s in range(4):
                xs[q * 4 + s, 0:height, lanes] = pick([tiles[(l - s) % 4] for l in range(4)])

    def spread(piece, groups_of):
        width = 128 * len(groups_of)
        xs = xs0 if piece == 0 else xs1
        shifts = [[jnp.full((16, 1024), (8 * o).astype(F32)).astype(BF) for o in owners] for owners in groups_of]

        @pl.loop(0, 8)
        def _(q):
            for s in range(4):
                slab = q * 4 + s
                w16 = xs0[slab, COLS : COLS + 16, :]
                lab16 = xs0[slab, COLS + 16 : COLS + 32, :]
                for n, shift in enumerate(shifts):
                    lab = [lab16 - shift[0], lab16 - shift[1]]
                    for i in range(8):
                        a = (i // 2 - s) % 4
                        mine = 4 * (a % 2) + 2 * (i % 2)
                        st[s, n * 128 + i * 16 : n * 128 + i * 16 + 16, :] = jnp.where(
                            lab[a // 2] == jnp.full_like(w16, mine), w16, jnp.zeros_like(w16)
                        )
                vt[s, :, 0:width] = lax.dot_general(xs[slab, 0:COLS, :], st[s, 0:width, :], NT, preferred_element_type=F32)
            for n, owners in enumerate(groups_of):
                tiles = [vt[s, :, n * 128 : n * 128 + 128] for s in range(4)]
                for a in range(4):
                    vol[piece, owners[a // 2], (a % 2) * 8 + q] = pick([tiles[(l - a) % 4] for l in range(4)])

    ring = {}

    def hop(piece, chain, t, parts=(0, 1)):
        buf, ssem, rsem = ((ra, sa, ka), (rb, sb, kb))[chain]
        for part in parts:
            sign = (1 if part == 0 else -1) * (1 if chain == 0 else -1)
            owner = lax.rem(g + sign * (4 - chain - t + 1) + NG, NG)
            mine = vol.at[piece, owner, pl.ds(part * 8, 8)]
            if t == 1:
                src = mine
            else:
                ring[piece, chain, t - 1, part].wait_recv()
                src = buf.at[piece, part, t - 2]
                src[...] += mine[...]
            copy = pltpu.make_async_remote_copy(
                src, buf.at[piece, part, t - 1], ssem.at[piece, part, t - 1], rsem.at[piece, part, t - 1],
                device_id={"grp": lax.rem(g + sign + NG, NG)}, device_id_type=MESH,
            )
            copy.start()
            ring[piece, chain, t, part] = copy

    def image(piece):
        for part in range(2):
            ring[piece, 1, 3, part].wait_recv()
            ring[piece, 0, 4, part].wait_recv()
        lam = taucol[pl.ds(pl.multiple_of(lax.rem(me, 4) * 32 + piece * KX, 16), KX), :]
        for part in range(2):
            shift = lax.rem(128 - 32 * (2 * (g & 1) + part), 128)
            for q in range(8):
                tile = vol[piece, g, part * 8 + q] + ra[piece, part, 3, q] + rb[piece, part, 2, q]
                scale = tile[2 * KX : 3 * KX] + lam
                for c in range(2):
                    f = pltpu.roll(tile[c * KX : c * KX + KX] / scale, shift, 1)
                    hi = f.astype(BF)
                    r = c * 32 + part * KX
                    lhs[r : r + KX, q * 128 : q * 128 + 128] = hi
                    lhs[64 + r : 64 + r + KX, q * 128 : q * 128 + 128] = (f - hi.astype(F32)).astype(BF)

        def product(first):
            cols = slice(first, first + 256)
            full = jnp.dot(lhs[...], wh[:, cols], preferred_element_type=F32)
            return full[0:64] + full[64:128] + jnp.dot(lhs[0:64, :], wl[:, cols], preferred_element_type=F32)

        for n in range(4):
            c = product(n * 256)
            s = product(1024 + n * 256)
            for part in range(2):
                rows = slice(part * 32 + piece * KX, part * 32 + piece * KX + KX)
                low, high = slice(part * KX, part * KX + KX), slice(32 + part * KX, 32 + part * KX + KX)
                out[0, rows, n * 256 : n * 256 + 256] = c[low] - s[high]
                out[1, rows, n * 256 : n * 256 + 256] = s[low] + c[high]

    def owners(i, j):
        first, second = lax.rem(g + i, NG), lax.rem(g + j, NG)
        odd = first & 1
        return (first + odd * (second - first), second + odd * (first - second))

    pairs = [owners(4, 3), owners(5, 2), owners(6, 1), owners(7, 0)]

    def places(piece, first, last):
        @pl.loop(first, last)
        def _(step):
            place(piece, step)

    places(0, 0, 4)
    for step in range(4):
        send(1, step)
    places(0, 4, 6)
    for step in range(4, 6):
        send(1, step)
    places(0, 6, 8)
    for step in range(6, 8):
        send(1, step)
    spread(0, pairs[0:1])
    hop(0, 0, 1)
    hop(0, 1, 1, (1,))
    spread(0, pairs[1:2])
    hop(0, 1, 1, (0,))
    places(1, 0, 2)
    hop(0, 0, 2)
    spread(0, pairs[2:3])
    hop(0, 1, 2)
    spread(0, pairs[3:4])
    hop(0, 0, 3)
    places(1, 2, 4)
    hop(0, 1, 3)
    places(1, 4, 6)
    hop(0, 0, 4)
    places(1, 6, 8)
    spread(1, pairs[0:1])
    hop(1, 0, 1)
    hop(1, 1, 1, (1,))
    spread(1, pairs[1:2])
    hop(1, 1, 1, (0,))
    hop(1, 0, 2)
    spread(1, pairs[2:3])
    hop(1, 1, 2)
    spread(1, pairs[3:4])
    hop(1, 0, 3)
    tables()
    hop(1, 1, 3)
    image(0)
    hop(1, 0, 4)
    image(1)
    for copy in sends:
        copy.wait_send()
    for copy in ring.values():
        copy.wait_send()


def factors():
    z = np.arange(1024)
    digit = np.arange(32)[:, None]
    coarse = 2.0 * math.pi * (32 * digit * z % 1024) / 1024
    fine = 2.0 * math.pi * (digit * z % 1024) / 1024
    scale = 1.0 / 32.0
    return [np.asarray(a, np.float32) for a in (np.cos(coarse), np.sin(coarse), scale * np.cos(fine), scale * np.sin(fine))]


def on_device(spectra, ctf_sq, dest, block, pattern, pattern_table, tau):
    iota = jnp.asarray(np.tile(np.arange(256)[:, None], (1, 128)), BF)
    groups = jnp.asarray(np.tile(np.arange(128)[None, :] // 32, (128, 1)), BF)
    dma = pltpu.SemaphoreType.DMA
    small = (
        dest.reshape(1, ROWS), block.reshape(1, ROWS), pattern.reshape(1, ROWS), tau.reshape(1, 1024),
        iota, pattern_table.T, groups, *[jnp.asarray(a) for a in factors()],
    )
    operands = (spectra, ctf_sq, *small)
    image = pl.pallas_call(
        kernel,
        out_shape=jax.ShapeDtypeStruct((2, 64, 1024), F32),
        in_specs=[pl.BlockSpec(memory_space=pl.ANY)] * len(operands),
        out_specs=pl.BlockSpec(memory_space=pltpu.VMEM),
        scratch_shapes=[
            pltpu.VMEM((4, 3, ROWS, 256), BF),
            *[pltpu.VMEM(a.shape, a.dtype) for a in small],
            pltpu.VMEM((NS, 13, 16, 128), BF),
            pltpu.VMEM((NS, 12, 16, 128), BF),
            pltpu.VMEM((NS, 13, 16, 128), BF),
            pltpu.VMEM((NS, 12, 16, 128), BF),
            pltpu.VMEM((16, ROWS), F32),
            pltpu.VMEM((ROWS, ROWS), BF),
            pltpu.VMEM((16, 128), F32),
            pltpu.VMEM((COLS + 32, ROWS), BF),
            pltpu.VMEM((2, 256, ROWS), BF),
            pltpu.VMEM((4, COLS + 32, 1024), BF),
            pltpu.VMEM((NS, COLS + 32, 1024), BF),
            pltpu.VMEM((NS, COLS, 1024), BF),
            pltpu.VMEM((4, 256, 1024), BF),
            pltpu.VMEM((4, COLS, 256), F32),
            pltpu.VMEM((PIECES, NG, 16, COLS, 128), F32),
            pltpu.VMEM((PIECES, 2, 4, 8, COLS, 128), F32),
            pltpu.VMEM((PIECES, 2, 3, 8, COLS, 128), F32),
            pltpu.VMEM((1024, 2048), BF),
            pltpu.VMEM((1024, 2048), BF),
            pltpu.VMEM((128, 1024), BF),
            pltpu.VMEM((128, 128), F32),
            dma((4, 3)),
            dma((SMALL,)),
            dma((NS,)),
            dma((NS,)),
            dma((NS,)),
            dma((NS,)),
            dma((PIECES, 2, 4)),
            dma((PIECES, 2, 4)),
            dma((PIECES, 2, 3)),
            dma((PIECES, 2, 3)),
        ],
        compiler_params=pltpu.CompilerParams(
            collective_id=0, has_side_effects=True, vmem_limit_bytes=62 * 1024 * 1024
        ),
        name="backproject",
    )(*operands)
    return jnp.transpose(image.reshape(2, 2, 32, 1024), (0, 1, 3, 2))


def solution(mesh):
    rows = P(("grp", "slab"))
    wide = P(("grp", "slab"), None)
    return jax.shard_map(
        on_device,
        mesh=mesh,
        in_specs=(wide, wide, wide, rows, rows, P(), P()),
        out_specs=P(None, "grp", None, "slab"),
        check_vma=False,
    )
```
